32 devices in a mesh: leaf: 4 (over z), bits: 8 (over y, x, core).
Axes of the slice: x: 2, y: 2, z: 4, core: 2. Of those that a mesh axis runs over, the one named last changes fastest.
Arguments:
- state: float32 [2, 4, 8, 4096, 256], P(None, 'leaf', 'bits'), may hold values from -6 to 6
- gate_one: float32 [2, 512, 512], replicated, may hold values from -0.1875 to 0.1875
- gate_two: float32 [2, 512, 512], replicated, may hold values from -0.1875 to 0.1875
- row_order: int32 [4096], replicated, may hold values from 0 to 4095, each once
- picks: int32 [8, 4096], P('bits'), may hold values from 0 to 4095, each once within a row
- counts: int32 [8, 4096], P('bits'), may hold values from 1 to 256, as said below
Outputs:
- amplitudes: float32 [2, 8, 4096, 256], P(None, 'bits', 'leaf')
The draws below stay inside these ranges and needn't reach their ends.
Inputs may be any that keep to these rules, and one draw needn't show every extreme that they name: `counts`: live columns of each block; the first block of every group holds 256. `picks`: each group's blocks name every row once.
All inputs are finite; a program needn't handle non-finite values.
Results may differ from the reference program's by a relative error of at most 0.0001.
Values sent between devices are 32-bit elements; how exact they have to be, the bound alone decides.
A program may use at most 128 MiB of HBM per device.

```python
import jax
import jax.numpy as jnp
from jax import lax

K = 256
R_DEV = 4096
SWAP_ONE = 0
SWAP_TWO = 2
N_LEAF = 4
N_BITS = 8


def draw_counts(key, part):
    values = jax.random.randint(key, (N_BITS, R_DEV), 1, K + 1)
    return values.at[:, 0].set(K).astype(jnp.int32)


def block_levels(rng, shape, shards, smallest, largest):
    def one(dim, blocks):
        heights = jax.random.uniform(jax.random.fold_in(jax.random.fold_in(rng, 6), dim), (blocks,), jnp.float32, smallest / len(shards), largest / len(shards))
        return jnp.repeat(jnp.exp(heights), shape[dim] // blocks).reshape((-1,) + (1,) * (len(shape) - dim - 1))

    loudness = one(*shards[0])
    for cut in shards[1:]:
        loudness = loudness * one(*cut)
    return loudness


def centred(rng, dims, spread, most, pieces=(), kind=jnp.bfloat16):
    level = block_levels(rng, dims, pieces, -0.22, 0.18) if pieces else 1.0
    array = jax.random.normal(rng, dims, jnp.float32) * spread * level
    return jnp.minimum(jnp.maximum(array, -most), most).astype(kind)


def setup_inputs(seed: int = 0) -> dict:
    arg_keys = jax.random.split(jax.random.key(seed), 7)
    state = centred(arg_keys[0], (2, N_LEAF, N_BITS, R_DEV, K), 1.0, 6.0, ((1, 4), (2, 8)), jnp.float32)
    gate_one = centred(arg_keys[1], (2, 2 * K, 2 * K), (4 * K) ** -0.5, 0.1875, (), jnp.float32)
    gate_two = centred(arg_keys[2], (2, 2 * K, 2 * K), (4 * K) ** -0.5, 0.1875, (), jnp.float32)
    row_order = jax.random.permutation(arg_keys[3], R_DEV).astype(jnp.int32)
    picks = jax.vmap(lambda own: jax.random.permutation(own, R_DEV))(jax.random.split(arg_keys[4], N_BITS)).reshape((N_BITS, R_DEV)).astype(jnp.int32)
    counts = draw_counts(jax.random.fold_in(arg_keys[6], 71), 0)
    return {"state": state, "gate_one": gate_one, "gate_two": gate_two, "row_order": row_order, "picks": picks, "counts": counts}


def complex_product(values, weights):
    highest = lax.Precision.HIGHEST
    real = jnp.einsum("...k,kn->...n", values[0], weights[0], precision=highest) - jnp.einsum("...k,kn->...n", values[1], weights[1], precision=highest)
    imaginary = jnp.einsum("...k,kn->...n", values[0], weights[1], precision=highest) + jnp.einsum("...k,kn->...n", values[1], weights[0], precision=highest)
    return jnp.stack([real, imaginary])


def quarter(gate, row_half, col_half):
    return gate[:, row_half * K:(row_half + 1) * K, col_half * K:(col_half + 1) * K]


def section_rows(state, gate_one, group_index, rows):
    high = (group_index >> SWAP_ONE) & 1
    mine_rows = state[:, :, group_index][:, :, rows]
    other_rows = state[:, :, group_index ^ (1 << SWAP_ONE)][:, :, rows]
    return complex_product(mine_rows, quarter(gate_one, high, high)) + complex_product(other_rows, quarter(gate_one, 1 - high, high))


def reference(state, gate_one, gate_two, row_order, picks, counts):
    results = []
    for group_index in range(N_BITS):
        rows = jnp.take(row_order, picks[group_index], axis=0).astype(jnp.int32)
        high = (group_index >> SWAP_TWO) & 1
        mine_section = section_rows(state, gate_one, group_index, rows)
        other_section = section_rows(state, gate_one, group_index ^ (1 << SWAP_TWO), rows)
        part = complex_product(mine_section, quarter(gate_two, high, high)) + complex_product(other_section, quarter(gate_two, 1 - high, high))
        summed = jnp.sum(part, axis=1)
        keep_mask = jnp.arange(K, dtype=jnp.int32)[None, :] < counts[group_index][:, None]
        results.append(jnp.where(keep_mask[None], summed, jnp.zeros_like(summed)))
    return jnp.stack(results, axis=1)
```

```python
import functools

import jax
import jax.numpy as jnp
from jax import lax
from jax.experimental import pallas as pl
from jax.experimental.pallas import tpu as pltpu
from jax.sharding import PartitionSpec as P

SWAP_ONE = 0
SWAP_TWO = 2
GROUPS = 2
PER_GROUP = 2
MESH = pl.DeviceIdType.MESH


def split(x):
    hi = x.astype(jnp.bfloat16)
    lo = (x - hi.astype(jnp.float32)).astype(jnp.bfloat16)
    return hi, lo


def kernel(
    n_leaf, picks_ref, order_ref, state_ref, one_ref, two_ref, out_ref,
    st, rs, ssum, core, sec, ybuf, parts, quarters, w_hi, w_lo,
    local_sem, rs_send, rs_recv, core_send, core_recv, y_send, y_recv, ag_send, ag_recv,
):
    me = lax.axis_index("leaf")
    group = lax.axis_index("bits")
    columns = state_ref.shape[2]
    block = state_ref.shape[1] // n_leaf
    chunks = GROUPS * PER_GROUP
    tall = block // chunks
    rc = tall // 2
    steps = n_leaf - 1
    high_one = group // 2**SWAP_ONE % 2
    high_two = group // 2**SWAP_TWO % 2
    partner_one = group + 2**SWAP_ONE * (1 - 2 * high_one)
    partner_two = group + 2**SWAP_TWO * (1 - 2 * high_two)
    neighbour = [lax.rem(me + 1, n_leaf), lax.rem(me + n_leaf - 1, n_leaf)]

    barrier = pltpu.get_barrier_semaphore()
    for where in (
        {"leaf": neighbour[0]}, {"leaf": neighbour[1]}, {"bits": partner_one}, {"bits": partner_two},
    ):
        pl.semaphore_signal(barrier, inc=1, device_id=where, device_id_type=MESH)
    load = pltpu.make_async_copy(state_ref, st, local_sem.at[0])
    load.start()
    loads = []
    for gate, ref, high in ((0, one_ref, high_one), (1, two_ref, high_two)):
        for other in range(2):
            row_half = high if other == 0 else 1 - high
            loads.append(
                pltpu.make_async_copy(
                    ref.at[:, pl.ds(pl.multiple_of(row_half * columns, columns), columns),
                           pl.ds(pl.multiple_of(high * columns, columns), columns)],
                    quarters.at[gate, other],
                    local_sem.at[1 + 2 * gate + other],
                )
            )
            loads[-1].start()
    pl.semaphore_wait(barrier, 4)

    def rows_of(b, c, d):
        b = lax.rem(b + 2 * n_leaf, n_leaf)
        return pl.ds(pl.multiple_of(b * block + c * tall + d * rc, rc), rc)

    def away(d, k):
        return me - k if d == 0 else me + k

    def rs_copy(d, s, c):
        if isinstance(s, int) and s == 0:
            src = state_ref.at[:, rows_of(away(d, 1), c, d), :]
        else:
            src = rs.at[d, s - 1, c]
        return pltpu.make_async_remote_copy(
            src_ref=src, dst_ref=rs.at[d, s, c],
            send_sem=rs_send.at[d, s, c], recv_sem=rs_recv.at[d, s, c],
            device_id={"leaf": neighbour[d]}, device_id_type=MESH,
        )

    def rs_arrival(d, s, c):
        piece = rs.at[d, s, c]
        return pltpu.make_async_remote_copy(
            src_ref=piece, dst_ref=piece,
            send_sem=rs_send.at[d, s, c], recv_sem=rs_recv.at[d, s, c],
            device_id={"leaf": neighbour[d]}, device_id_type=MESH,
        )

    def core_copy(c):
        return pltpu.make_async_remote_copy(
            src_ref=ssum.at[c], dst_ref=core.at[c],
            send_sem=core_send.at[c], recv_sem=core_recv.at[c],
            device_id={"bits": partner_one}, device_id_type=MESH,
        )

    def y_copy(c):
        return pltpu.make_async_remote_copy(
            src_ref=sec.at[c], dst_ref=ybuf.at[c],
            send_sem=y_send.at[c], recv_sem=y_recv.at[c],
            device_id={"bits": partner_two}, device_id_type=MESH,
        )

    def ag_copy(d, t, c):
        piece = parts.at[:, rows_of(away(d, t), c, d), :]
        return pltpu.make_async_remote_copy(
            src_ref=piece, dst_ref=piece,
            send_sem=ag_send.at[d, t, c], recv_sem=ag_recv.at[d, t, c],
            device_id={"leaf": neighbour[d]}, device_id_type=MESH,
        )

    def ag_arrival(d, t, c):
        piece = parts.at[:, rows_of(away(d, t + 1), c, d), :]
        return pltpu.make_async_remote_copy(
            src_ref=piece, dst_ref=piece,
            send_sem=ag_send.at[d, t, c], recv_sem=ag_recv.at[d, t, c],
            device_id={"leaf": neighbour[d]}, device_id_type=MESH,
        )

    def each(count, body):
        def step(i, carry):
            body(i)
            return carry

        lax.fori_loop(0, count, step, 0)

    def product(gate, mine, theirs):
        x = jnp.concatenate([mine[0], mine[1], theirs[0], theirs[1]], axis=1)
        x_hi, x_lo = split(x)
        dot = functools.partial(jnp.dot, preferred_element_type=jnp.float32)
        return dot(x_hi, w_hi[gate]) + (dot(x_lo, w_hi[gate]) + dot(x_hi, w_lo[gate]))

    def begin(g):
        for k in range(PER_GROUP):
            for d in range(2):
                rs_copy(d, 0, g * PER_GROUP + k).start()

    begin(0)

    for one in loads:
        one.wait()
    for gate in range(2):
        for other in range(2):
            re_hi, re_lo = split(quarters[gate, other, 0])
            im_hi, im_lo = split(quarters[gate, other, 1])
            top = pl.ds(2 * other * columns, columns)
            low = pl.ds((2 * other + 1) * columns, columns)
            left, right = pl.ds(0, columns), pl.ds(columns, columns)
            for w, re, im in ((w_hi, re_hi, im_hi), (w_lo, re_lo, im_lo)):
                w[gate, top, left] = re
                w[gate, top, right] = im
                w[gate, low, left] = -im
                w[gate, low, right] = re
    load.wait()

    def iteration(g):
        first = g * PER_GROUP

        @pl.when(g < GROUPS)
        def _():
            def forward(i):
                s, c = i // PER_GROUP, first + i % PER_GROUP
                for d in range(2):
                    rs_arrival(d, s, c).wait_recv()
                    rs[d, s, c] = rs[d, s, c] + st[:, rows_of(away(d, s + 2), c, d), :]
                    rs_copy(d, s + 1, c).start()

            each((steps - 1) * PER_GROUP, forward)

        @pl.when(g + 1 < GROUPS)
        def _():
            begin(g + 1)

        @pl.when((g >= 2) & (g < GROUPS + 2))
        def _():
            def forward(i):
                t, c = i // PER_GROUP, first - 2 * PER_GROUP + i % PER_GROUP
                for d in range(2):
                    ag_arrival(d, t, c).wait_recv()
                    ag_copy(d, t + 1, c).start()

            each((steps - 1) * PER_GROUP, forward)

        @pl.when((g >= 1) & (g < GROUPS + 1))
        def _():
            def second(k):
                c = first - PER_GROUP + k
                y_copy(c).wait_recv()
                part = product(1, sec[c], ybuf[c])
                here = pl.ds(pl.multiple_of(me * block + c * tall, tall), tall)
                parts[0, here, :] = part[:, :columns]
                parts[1, here, :] = part[:, columns:]
                for d in range(2):
                    ag_copy(d, 0, c).start()

            each(PER_GROUP, second)

        @pl.when(g < GROUPS)
        def _():
            def last(k):
                c = first + k
                for d in range(2):
                    rs_arrival(d, steps - 1, c).wait_recv()
                    ssum[c, :, pl.ds(d * rc, rc), :] = rs[d, steps - 1, c] + st[:, rows_of(me, c, d), :]
                core_copy(c).start()

            def first_step(k):
                c = first + k
                core_copy(c).wait_recv()
                section = product(0, ssum[c], core[c])
                sec[c, 0] = section[:, :columns]
                sec[c, 1] = section[:, columns:]
                y_copy(c).start()

            each(PER_GROUP, last)
            each(PER_GROUP, first_step)

    each(GROUPS + 2, iteration)

    def arrive(c):
        for d in range(2):
            ag_arrival(d, steps - 1, c).wait_recv()

    each(chunks, arrive)

    base = me * block
    unroll = 16

    def pick(i):
        for k in range(unroll):
            p = i * unroll + k
            row = order_ref[picks_ref[0, base + p]]
            out_ref[:, pl.ds(p, 1), :] = parts[:, pl.ds(row, 1), :]

    each(block // unroll, pick)

    def drain(c):
        for d in range(2):
            for s in range(steps):
                rs_copy(d, s, c).wait_send()
                ag_copy(d, s, c).wait_send()
        core_copy(c).wait_send()
        y_copy(c).wait_send()

    each(chunks, drain)


def shards(state, gate_one, gate_two, row_order, picks, counts):
    rows, columns = state.shape[-2:]
    n_leaf = lax.axis_size("leaf")
    block = rows // n_leaf
    chunks = GROUPS * PER_GROUP
    tall = block // chunks
    rc = tall // 2
    steps = n_leaf - 1
    f32, dma = jnp.float32, pltpu.SemaphoreType.DMA
    vmem, smem, hbm = (
        pl.BlockSpec(memory_space=m) for m in (pltpu.VMEM, pltpu.SMEM, pl.ANY)
    )
    picked = pl.pallas_call(
        functools.partial(kernel, n_leaf),
        out_shape=jax.ShapeDtypeStruct((2, block, columns), f32),
        in_specs=[smem, smem, hbm, hbm, hbm],
        out_specs=vmem,
        scratch_shapes=[
            pltpu.VMEM((2, rows, columns), f32),
            pltpu.VMEM((2, steps, chunks, 2, rc, columns), f32),
            pltpu.VMEM((chunks, 2, tall, columns), f32),
            pltpu.VMEM((chunks, 2, tall, columns), f32),
            pltpu.VMEM((chunks, 2, tall, columns), f32),
            pltpu.VMEM((chunks, 2, tall, columns), f32),
            pltpu.VMEM((2, rows, columns), f32),
            pltpu.VMEM((2, 2, 2, columns, columns), f32),
            pltpu.VMEM((2, 4 * columns, 2 * columns), jnp.bfloat16),
            pltpu.VMEM((2, 4 * columns, 2 * columns), jnp.bfloat16),
            dma((5,)),
            dma((2, steps, chunks)),
            dma((2, steps, chunks)),
            dma((chunks,)),
            dma((chunks,)),
            dma((chunks,)),
            dma((chunks,)),
            dma((2, steps, chunks)),
            dma((2, steps, chunks)),
        ],
        compiler_params=pltpu.CompilerParams(
            collective_id=0, has_side_effects=True, vmem_limit_bytes=60 * 2**20
        ),
    )(picks, row_order, state[:, 0, 0], gate_one, gate_two)
    live_counts = lax.dynamic_slice_in_dim(counts[0], lax.axis_index("leaf") * block, block)
    keep_mask = jnp.arange(columns, dtype=jnp.int32)[None, :] < live_counts[:, None]
    return jnp.where(keep_mask[None], picked, jnp.zeros_like(picked))[:, None]


def solution(mesh):
    return jax.shard_map(
        shards,
        mesh=mesh,
        in_specs=(
            P(None, "leaf", "bits", None, None),
            P(),
            P(),
            P(),
            P("bits", None),
            P("bits", None),
        ),
        out_specs=P(None, "bits", "leaf", None),
        check_vma=False,
    )
```

```python
import functools

import jax
import jax.numpy as jnp
from jax import lax
from jax.experimental import pallas as pl
from jax.experimental.pallas import tpu as pltpu
from jax.sharding import PartitionSpec as P

SWAP_ONE = 0
SWAP_TWO = 2
CHUNKS = 8
MESH = pl.DeviceIdType.MESH


def split(x):
    hi = x.astype(jnp.bfloat16)
    lo = (x - hi.astype(jnp.float32)).astype(jnp.bfloat16)
    return hi, lo


def kernel(
    n_leaf, picks_ref, order_ref, state_ref, one_ref, two_ref, out_ref,
    st, rs, ssum, core, sec, ybuf, parts, quarters, w_hi, w_lo,
    local_sem, rs_send, rs_recv, core_send, core_recv, y_send, y_recv, ag_send, ag_recv,
):
    me = lax.axis_index("leaf")
    group = lax.axis_index("bits")
    columns = state_ref.shape[2]
    block = state_ref.shape[1] // n_leaf
    tall = block // CHUNKS
    final = n_leaf - 1
    inner = (me > 0) & (me < final)
    high_one = group // 2**SWAP_ONE % 2
    high_two = group // 2**SWAP_TWO % 2
    partner_one = group + 2**SWAP_ONE * (1 - 2 * high_one)
    partner_two = group + 2**SWAP_TWO * (1 - 2 * high_two)
    neighbour = [lax.rem(me + 1, n_leaf), lax.rem(me + n_leaf - 1, n_leaf)]
    has = [me < final, me > 0]

    barrier = pltpu.get_barrier_semaphore()
    for d in range(2):

        @pl.when(has[d])
        def _():
            pl.semaphore_signal(
                barrier, inc=1, device_id={"leaf": neighbour[d]}, device_id_type=MESH
            )

    for partner in (partner_one, partner_two):
        pl.semaphore_signal(barrier, inc=1, device_id={"bits": partner}, device_id_type=MESH)
    load = pltpu.make_async_copy(state_ref, st, local_sem.at[0])
    load.start()
    loads = []
    for gate, ref, high in ((0, one_ref, high_one), (1, two_ref, high_two)):
        for other in range(2):
            row_half = high if other == 0 else 1 - high
            loads.append(
                pltpu.make_async_copy(
                    ref.at[:, pl.ds(pl.multiple_of(row_half * columns, columns), columns),
                           pl.ds(pl.multiple_of(high * columns, columns), columns)],
                    quarters.at[gate, other],
                    local_sem.at[1 + 2 * gate + other],
                )
            )
            loads[-1].start()

    @pl.when(inner)
    def _():
        pl.semaphore_wait(barrier, 4)

    @pl.when(jnp.logical_not(inner))
    def _():
        pl.semaphore_wait(barrier, 3)


    def rows_of(j, c):
        return pl.ds(pl.multiple_of(j * block + c * tall, tall), tall)

    def rs_copy(d, j, c, src=None):
        return pltpu.make_async_remote_copy(
            src_ref=rs.at[d, j, c] if src is None else src, dst_ref=rs.at[d, j, c],
            send_sem=rs_send.at[d, j, c], recv_sem=rs_recv.at[d, j, c],
            device_id={"leaf": neighbour[d]}, device_id_type=MESH,
        )

    def core_copy(c):
        return pltpu.make_async_remote_copy(
            src_ref=ssum.at[c], dst_ref=core.at[c],
            send_sem=core_send.at[c], recv_sem=core_recv.at[c],
            device_id={"bits": partner_one}, device_id_type=MESH,
        )

    def y_copy(c):
        return pltpu.make_async_remote_copy(
            src_ref=sec.at[c], dst_ref=ybuf.at[c],
            send_sem=y_send.at[c], recv_sem=y_recv.at[c],
            device_id={"bits": partner_two}, device_id_type=MESH,
        )

    def ag_copy(d, j, c):
        piece = parts.at[:, rows_of(j, c), :]
        return pltpu.make_async_remote_copy(
            src_ref=piece, dst_ref=piece,
            send_sem=ag_send.at[d, j, c], recv_sem=ag_recv.at[d, j, c],
            device_id={"leaf": neighbour[d]}, device_id_type=MESH,
        )

    def each(count, body):
        def step(i, carry):
            body(i)
            return carry

        lax.fori_loop(0, count, step, 0)

    def product(gate, mine, theirs):
        x = jnp.concatenate([mine[0], mine[1], theirs[0], theirs[1]], axis=1)
        x_hi, x_lo = split(x)
        dot = functools.partial(jnp.dot, preferred_element_type=jnp.float32)
        return dot(x_hi, w_hi[gate]) + (dot(x_lo, w_hi[gate]) + dot(x_hi, w_lo[gate]))

    @pl.when(me == 0)
    def _():
        def begin(i):
            c, j = i // final, final - i % final
            rs_copy(0, j, c, state_ref.at[:, rows_of(j, c), :]).start()

        each(CHUNKS * final, begin)

    @pl.when(me == final)
    def _():
        def begin(i):
            c, j = i // final, i % final
            rs_copy(1, j, c, state_ref.at[:, rows_of(j, c), :]).start()

        each(CHUNKS * final, begin)

    for one in loads:
        one.wait()
    for gate in range(2):
        for other in range(2):
            re_hi, re_lo = split(quarters[gate, other, 0])
            im_hi, im_lo = split(quarters[gate, other, 1])
            top = pl.ds(2 * other * columns, columns)
            low = pl.ds((2 * other + 1) * columns, columns)
            left, right = pl.ds(0, columns), pl.ds(columns, columns)
            for w, re, im in ((w_hi, re_hi, im_hi), (w_lo, re_lo, im_lo)):
                w[gate, top, left] = re
                w[gate, top, right] = im
                w[gate, low, left] = -im
                w[gate, low, right] = re
    load.wait()

    def reduce_on(c):
        def toward(k):
            for d, j, ahead in ((0, final - k, final - k > me), (1, k, k < me)):

                @pl.when(inner & ahead)
                def _():
                    rs_copy(d, j, c).wait_recv()
                    rs[d, j, c] = rs[d, j, c] + st[:, rows_of(j, c), :]
                    rs_copy(d, j, c).start()

        each(final, toward)

    def gather_near(c):
        for d, j, there in (
            (0, me - 1, (me < final) & (me > 1)), (1, me + 1, (me > 0) & (me < final - 1))
        ):

            @pl.when(there)
            def _():
                ag_copy(d, j, c).wait_recv()
                ag_copy(d, j, c).start()

    def second_step(c):
        y_copy(c).wait_recv()
        part = product(1, sec[c], ybuf[c])
        here = rows_of(me, c)
        parts[0, here, :] = part[:, :columns]
        parts[1, here, :] = part[:, columns:]
        for d in range(2):

            @pl.when(has[d])
            def _():
                ag_copy(d, me, c).start()

    def own_sum(c):
        @pl.when(me > 0)
        def _():
            rs_copy(0, me, c).wait_recv()

        @pl.when(me < final)
        def _():
            rs_copy(1, me, c).wait_recv()

        mine = rows_of(me, c)

        @pl.when(me == 0)
        def _():
            ssum[c] = st[:, mine, :] + rs[1, me, c]

        @pl.when(me == final)
        def _():
            ssum[c] = st[:, mine, :] + rs[0, me, c]

        @pl.when(inner)
        def _():
            ssum[c] = st[:, mine, :] + rs[0, me, c] + rs[1, me, c]

        core_copy(c).start()

    def first_step(c):
        core_copy(c).wait_recv()
        section = product(0, ssum[c], core[c])
        sec[c, 0] = section[:, :columns]
        sec[c, 1] = section[:, columns:]
        y_copy(c).start()

    def iteration(g):
        @pl.when(g < CHUNKS)
        def _():
            reduce_on(g)
            own_sum(g)

        @pl.when(g >= 2)
        def _():
            gather_near(g - 2)

        @pl.when(g < CHUNKS)
        def _():
            first_step(g)

        @pl.when((g >= 1) & (g < CHUNKS + 1))
        def _():
            second_step(g - 1)

    each(CHUNKS + 2, iteration)

    def gather_rest(i):
        c, k = i // n_leaf, i % n_leaf
        late = (k < me) & ((k < me - 1) | (k == 0) | (me == final))

        @pl.when(late)
        def _():
            ag_copy(0, k, c).wait_recv()

            @pl.when(me < final)
            def _():
                ag_copy(0, k, c).start()

        late_right = (k > me) & ((k > me + 1) | (k == final) | (me == 0))

        @pl.when(late_right)
        def _():
            ag_copy(1, k, c).wait_recv()

            @pl.when(me > 0)
            def _():
                ag_copy(1, k, c).start()

    each(CHUNKS * n_leaf, gather_rest)

    base = me * block
    unroll = 16

    def pick(i):
        for k in range(unroll):
            p = i * unroll + k
            row = order_ref[picks_ref[0, base + p]]
            out_ref[:, pl.ds(p, 1), :] = parts[:, pl.ds(row, 1), :]

    each(block // unroll, pick)

    def drain(i):
        c, j = i // n_leaf, i % n_leaf
        for d, sent, gathered in ((0, j > me, j <= me), (1, j < me, j >= me)):

            @pl.when(has[d] & sent)
            def _():
                rs_copy(d, j, c).wait_send()

            @pl.when(has[d] & gathered)
            def _():
                ag_copy(d, j, c).wait_send()

        @pl.when(j == 0)
        def _():
            core_copy(c).wait_send()
            y_copy(c).wait_send()

    each(CHUNKS * n_leaf, drain)


def shards(state, gate_one, gate_two, row_order, picks, counts):
    rows, columns = state.shape[-2:]
    n_leaf = lax.axis_size("leaf")
    block = rows // n_leaf
    tall = block // CHUNKS
    f32, dma = jnp.float32, pltpu.SemaphoreType.DMA
    vmem, smem, hbm = (
        pl.BlockSpec(memory_space=m) for m in (pltpu.VMEM, pltpu.SMEM, pl.ANY)
    )
    picked = pl.pallas_call(
        functools.partial(kernel, n_leaf),
        out_shape=jax.ShapeDtypeStruct((2, block, columns), f32),
        in_specs=[smem, smem, hbm, hbm, hbm],
        out_specs=vmem,
        scratch_shapes=[
            pltpu.VMEM((2, rows, columns), f32),
            pltpu.VMEM((2, n_leaf, CHUNKS, 2, tall, columns), f32),
            pltpu.VMEM((CHUNKS, 2, tall, columns), f32),
            pltpu.VMEM((CHUNKS, 2, tall, columns), f32),
            pltpu.VMEM((CHUNKS, 2, tall, columns), f32),
            pltpu.VMEM((CHUNKS, 2, tall, columns), f32),
            pltpu.VMEM((2, rows, columns), f32),
            pltpu.VMEM((2, 2, 2, columns, columns), f32),
            pltpu.VMEM((2, 4 * columns, 2 * columns), jnp.bfloat16),
            pltpu.VMEM((2, 4 * columns, 2 * columns), jnp.bfloat16),
            dma((5,)),
            dma((2, n_leaf, CHUNKS)),
            dma((2, n_leaf, CHUNKS)),
            dma((CHUNKS,)),
            dma((CHUNKS,)),
            dma((CHUNKS,)),
            dma((CHUNKS,)),
            dma((2, n_leaf, CHUNKS)),
            dma((2, n_leaf, CHUNKS)),
        ],
        compiler_params=pltpu.CompilerParams(
            collective_id=0, has_side_effects=True, vmem_limit_bytes=60 * 2**20
        ),
    )(picks, row_order, state[:, 0, 0], gate_one, gate_two)
    live_counts = lax.dynamic_slice_in_dim(counts[0], lax.axis_index("leaf") * block, block)
    keep_mask = jnp.arange(columns, dtype=jnp.int32)[None, :] < live_counts[:, None]
    return jnp.where(keep_mask[None], picked, jnp.zeros_like(picked))[:, None]


def solution(mesh):
    return jax.shard_map(
        shards,
        mesh=mesh,
        in_specs=(
            P(None, "leaf", "bits", None, None),
            P(),
            P(),
            P(),
            P("bits", None),
            P("bits", None),
        ),
        out_specs=P(None, "bits", "leaf", None),
        check_vma=False,
    )
```

```python
import functools

import jax
import jax.numpy as jnp
from jax import lax
from jax.experimental import pallas as pl
from jax.experimental.pallas import tpu as pltpu
from jax.sharding import PartitionSpec as P

SWAP_ONE = 0
SWAP_TWO = 2
CHUNKS = 16
MESH = pl.DeviceIdType.MESH


def split(x):
    hi = x.astype(jnp.bfloat16)
    lo = (x - hi.astype(jnp.float32)).astype(jnp.bfloat16)
    return hi, lo


def kernel(
    n_leaf, picks_ref, order_ref, state_ref, one_ref, two_ref, out_ref,
    st, rs, ssum, core, sec, ybuf, parts, quarters, w_hi, w_lo,
    local_sem, rs_send, rs_recv, core_send, core_recv, y_send, y_recv, ag_send, ag_recv,
):
    me = lax.axis_index("leaf")
    group = lax.axis_index("bits")
    columns = state_ref.shape[2]
    block = state_ref.shape[1] // n_leaf
    tall = block // CHUNKS
    final = n_leaf - 1
    hold = max(CHUNKS - final - 4, 0)
    inner = (me > 0) & (me < final)
    high_one = group // 2**SWAP_ONE % 2
    high_two = group // 2**SWAP_TWO % 2
    partner_one = group + 2**SWAP_ONE * (1 - 2 * high_one)
    partner_two = group + 2**SWAP_TWO * (1 - 2 * high_two)
    neighbour = [lax.rem(me + 1, n_leaf), lax.rem(me + n_leaf - 1, n_leaf)]
    has = [me < final, me > 0]

    barrier = pltpu.get_barrier_semaphore()
    for d in range(2):

        @pl.when(has[d])
        def _():
            pl.semaphore_signal(
                barrier, inc=1, device_id={"leaf": neighbour[d]}, device_id_type=MESH
            )

    for partner in (partner_one, partner_two):
        pl.semaphore_signal(barrier, inc=1, device_id={"bits": partner}, device_id_type=MESH)
    load = pltpu.make_async_copy(state_ref, st, local_sem.at[0])
    load.start()
    loads = []
    for gate, ref, high in ((0, one_ref, high_one), (1, two_ref, high_two)):
        for other in range(2):
            row_half = high if other == 0 else 1 - high
            loads.append(
                pltpu.make_async_copy(
                    ref.at[:, pl.ds(pl.multiple_of(row_half * columns, columns), columns),
                           pl.ds(pl.multiple_of(high * columns, columns), columns)],
                    quarters.at[gate, other],
                    local_sem.at[1 + 2 * gate + other],
                )
            )
            loads[-1].start()

    @pl.when(inner)
    def _():
        pl.semaphore_wait(barrier, 4)

    @pl.when(jnp.logical_not(inner))
    def _():
        pl.semaphore_wait(barrier, 3)


    def rows_of(j, c):
        return pl.ds(pl.multiple_of(j * block + c * tall, tall), tall)

    def rs_copy(d, j, c, src=None):
        return pltpu.make_async_remote_copy(
            src_ref=rs.at[d, j, c] if src is None else src, dst_ref=rs.at[d, j, c],
            send_sem=rs_send.at[d, j, c], recv_sem=rs_recv.at[d, j, c],
            device_id={"leaf": neighbour[d]}, device_id_type=MESH,
        )

    def core_copy(c):
        return pltpu.make_async_remote_copy(
            src_ref=ssum.at[c], dst_ref=core.at[c],
            send_sem=core_send.at[c], recv_sem=core_recv.at[c],
            device_id={"bits": partner_one}, device_id_type=MESH,
        )

    def y_copy(c):
        return pltpu.make_async_remote_copy(
            src_ref=sec.at[c], dst_ref=ybuf.at[c],
            send_sem=y_send.at[c], recv_sem=y_recv.at[c],
            device_id={"bits": partner_two}, device_id_type=MESH,
        )

    def ag_copy(d, j, c):
        piece = parts.at[:, rows_of(j, c), :]
        return pltpu.make_async_remote_copy(
            src_ref=piece, dst_ref=piece,
            send_sem=ag_send.at[d, j, c], recv_sem=ag_recv.at[d, j, c],
            device_id={"leaf": neighbour[d]}, device_id_type=MESH,
        )

    def each(count, body):
        def step(i, carry):
            body(i)
            return carry

        lax.fori_loop(0, count, step, 0)

    def product(gate, mine, theirs):
        x = jnp.concatenate([mine[0], mine[1], theirs[0], theirs[1]], axis=1)
        x_hi, x_lo = split(x)
        dot = functools.partial(jnp.dot, preferred_element_type=jnp.float32)
        return dot(x_hi, w_hi[gate]) + (dot(x_lo, w_hi[gate]) + dot(x_hi, w_lo[gate]))

    def begin(c):
        def send(k):
            @pl.when(me == 0)
            def _():
                rs_copy(0, final - k, c, state_ref.at[:, rows_of(final - k, c), :]).start()

            @pl.when(me == final)
            def _():
                rs_copy(1, k, c, state_ref.at[:, rows_of(k, c), :]).start()

        each(final, send)

    each(2, begin)

    for one in loads:
        one.wait()
    for gate in range(2):
        for other in range(2):
            re_hi, re_lo = split(quarters[gate, other, 0])
            im_hi, im_lo = split(quarters[gate, other, 1])
            top = pl.ds(2 * other * columns, columns)
            low = pl.ds((2 * other + 1) * columns, columns)
            left, right = pl.ds(0, columns), pl.ds(columns, columns)
            for w, re, im in ((w_hi, re_hi, im_hi), (w_lo, re_lo, im_lo)):
                w[gate, top, left] = re
                w[gate, top, right] = im
                w[gate, low, left] = -im
                w[gate, low, right] = re
    load.wait()

    def reduce_on(d, c):
        def toward(k):
            j, ahead = ((final - k, final - k > me), (k, k < me))[d]

            @pl.when(ahead)
            def _():
                rs_copy(d, j, c).wait_recv()
                rs[d, j, c] = rs[d, j, c] + st[:, rows_of(j, c), :]
                rs_copy(d, j, c).start()

        each(final, toward)

    def gather_near(c):
        for d, j, there in (
            (0, me - 1, (me < final) & (me > 1)), (1, me + 1, (me > 0) & (me < final - 1))
        ):

            @pl.when(there)
            def _():
                ag_copy(d, j, c).wait_recv()
                ag_copy(d, j, c).start()

    def gather_own(c):
        for d in range(2):

            @pl.when(has[d])
            def _():
                ag_copy(d, me, c).start()

    def second_step(c):
        y_copy(c).wait_recv()
        part = product(1, sec[c], ybuf[c])
        here = rows_of(me, c)
        parts[0, here, :] = part[:, :columns]
        parts[1, here, :] = part[:, columns:]

        @pl.when(inner | (c >= hold))
        def _():
            gather_own(c)

        @pl.when(jnp.logical_not(inner) & (c == hold))
        def _():
            each(hold, gather_own)

    def own_sum(c):
        @pl.when(me > 0)
        def _():
            rs_copy(0, me, c).wait_recv()

        @pl.when(me < final)
        def _():
            rs_copy(1, me, c).wait_recv()

        mine = rows_of(me, c)

        @pl.when(me == 0)
        def _():
            ssum[c] = st[:, mine, :] + rs[1, me, c]

        @pl.when(me == final)
        def _():
            ssum[c] = st[:, mine, :] + rs[0, me, c]

        @pl.when(inner)
        def _():
            ssum[c] = st[:, mine, :] + rs[0, me, c] + rs[1, me, c]

        core_copy(c).start()

    def first_step(c):
        core_copy(c).wait_recv()
        section = product(0, ssum[c], core[c])
        sec[c, 0] = section[:, :columns]
        sec[c, 1] = section[:, columns:]
        y_copy(c).start()

    def iteration(i):
        g = i - final

        @pl.when(i + 2 < CHUNKS)
        def _():
            begin(i + 2)

        @pl.when((g >= 0) & (g < CHUNKS))
        def _():
            own_sum(g)

        for d, c in ((0, g + final - me), (1, g + me)):

            @pl.when(inner & (c >= 0) & (c < CHUNKS))
            def _():
                reduce_on(d, c)

        @pl.when(g >= 3)
        def _():
            gather_near(g - 3)

        @pl.when((g >= 1) & (g < CHUNKS + 1))
        def _():
            second_step(g - 1)

        @pl.when((g >= 0) & (g < CHUNKS))
        def _():
            first_step(g)

    each(final + CHUNKS + 3, iteration)

    def gather_rest(i):
        c, k = i // n_leaf, i % n_leaf
        late = (k < me) & ((k < me - 1) | (k == 0) | (me == final))

        @pl.when(late)
        def _():
            ag_copy(0, k, c).wait_recv()

            @pl.when(me < final)
            def _():
                ag_copy(0, k, c).start()

        late_right = (k > me) & ((k > me + 1) | (k == final) | (me == 0))

        @pl.when(late_right)
        def _():
            ag_copy(1, k, c).wait_recv()

            @pl.when(me > 0)
            def _():
                ag_copy(1, k, c).start()

    each(CHUNKS * n_leaf, gather_rest)

    base = me * block
    unroll = 16

    def pick(i):
        for k in range(unroll):
            p = i * unroll + k
            row = order_ref[picks_ref[0, base + p]]
            out_ref[:, pl.ds(p, 1), :] = parts[:, pl.ds(row, 1), :]

    each(block // unroll, pick)

    def drain(i):
        c, j = i // n_leaf, i % n_leaf
        for d, sent, gathered in ((0, j > me, j <= me), (1, j < me, j >= me)):

            @pl.when(has[d] & sent)
            def _():
                rs_copy(d, j, c).wait_send()

            @pl.when(has[d] & gathered)
            def _():
                ag_copy(d, j, c).wait_send()

        @pl.when(j == 0)
        def _():
            core_copy(c).wait_send()
            y_copy(c).wait_send()

    each(CHUNKS * n_leaf, drain)


def shards(state, gate_one, gate_two, row_order, picks, counts):
    rows, columns = state.shape[-2:]
    n_leaf = lax.axis_size("leaf")
    block = rows // n_leaf
    tall = block // CHUNKS
    f32, dma = jnp.float32, pltpu.SemaphoreType.DMA
    vmem, smem, hbm = (
        pl.BlockSpec(memory_space=m) for m in (pltpu.VMEM, pltpu.SMEM, pl.ANY)
    )
    picked = pl.pallas_call(
        functools.partial(kernel, n_leaf),
        out_shape=jax.ShapeDtypeStruct((2, block, columns), f32),
        in_specs=[smem, smem, hbm, hbm, hbm],
        out_specs=vmem,
        scratch_shapes=[
            pltpu.VMEM((2, rows, columns), f32),
            pltpu.VMEM((2, n_leaf, CHUNKS, 2, tall, columns), f32),
            pltpu.VMEM((CHUNKS, 2, tall, columns), f32),
            pltpu.VMEM((CHUNKS, 2, tall, columns), f32),
            pltpu.VMEM((CHUNKS, 2, tall, columns), f32),
            pltpu.VMEM((CHUNKS, 2, tall, columns), f32),
            pltpu.VMEM((2, rows, columns), f32),
            pltpu.VMEM((2, 2, 2, columns, columns), f32),
            pltpu.VMEM((2, 4 * columns, 2 * columns), jnp.bfloat16),
            pltpu.VMEM((2, 4 * columns, 2 * columns), jnp.bfloat16),
            dma((5,)),
            dma((2, n_leaf, CHUNKS)),
            dma((2, n_leaf, CHUNKS)),
            dma((CHUNKS,)),
            dma((CHUNKS,)),
            dma((CHUNKS,)),
            dma((CHUNKS,)),
            dma((2, n_leaf, CHUNKS)),
            dma((2, n_leaf, CHUNKS)),
        ],
        compiler_params=pltpu.CompilerParams(
            collective_id=0, has_side_effects=True, vmem_limit_bytes=60 * 2**20
        ),
    )(picks, row_order, state[:, 0, 0], gate_one, gate_two)
    live_counts = lax.dynamic_slice_in_dim(counts[0], lax.axis_index("leaf") * block, block)
    keep_mask = jnp.arange(columns, dtype=jnp.int32)[None, :] < live_counts[:, None]
    return jnp.where(keep_mask[None], picked, jnp.zeros_like(picked))[:, None]


def solution(mesh):
    return jax.shard_map(
        shards,
        mesh=mesh,
        in_specs=(
            P(None, "leaf", "bits", None, None),
            P(),
            P(),
            P(),
            P("bits", None),
            P("bits", None),
        ),
        out_specs=P(None, "bits", "leaf", None),
        check_vma=False,
    )
```

```python
import functools

import jax
import jax.numpy as jnp
from jax import lax
from jax.experimental import pallas as pl
from jax.experimental.pallas import tpu as pltpu
from jax.sharding import PartitionSpec as P

SWAP_ONE = 0
SWAP_TWO = 2
CHUNKS = 16
MESH = pl.DeviceIdType.MESH


def split(x):
    hi = x.astype(jnp.bfloat16)
    lo = (x - hi.astype(jnp.float32)).astype(jnp.bfloat16)
    return hi, lo


def kernel(
    n_leaf, picks_ref, order_ref, state_ref, one_ref, two_ref, out_ref,
    st, rs, ssum, core, sec, ybuf, parts, quarters, w_hi, w_lo,
    local_sem, rs_send, rs_recv, core_send, core_recv, y_send, y_recv, ag_send, ag_recv,
):
    me = lax.axis_index("leaf")
    group = lax.axis_index("bits")
    columns = state_ref.shape[2]
    block = state_ref.shape[1] // n_leaf
    tall = block // CHUNKS
    final = n_leaf - 1
    hold = max(CHUNKS - final - 5, 0)
    inner = (me > 0) & (me < final)
    high_one = group // 2**SWAP_ONE % 2
    high_two = group // 2**SWAP_TWO % 2
    partner_one = group + 2**SWAP_ONE * (1 - 2 * high_one)
    partner_two = group + 2**SWAP_TWO * (1 - 2 * high_two)
    neighbour = [lax.rem(me + 1, n_leaf), lax.rem(me + n_leaf - 1, n_leaf)]
    has = [me < final, me > 0]

    barrier = pltpu.get_barrier_semaphore()
    for d in range(2):

        @pl.when(has[d])
        def _():
            pl.semaphore_signal(
                barrier, inc=1, device_id={"leaf": neighbour[d]}, device_id_type=MESH
            )

    for partner in (partner_one, partner_two):
        pl.semaphore_signal(barrier, inc=1, device_id={"bits": partner}, device_id_type=MESH)
    load = pltpu.make_async_copy(state_ref, st, local_sem.at[0])
    load.start()
    loads = []
    for gate, ref, high in ((0, one_ref, high_one), (1, two_ref, high_two)):
        for other in range(2):
            row_half = high if other == 0 else 1 - high
            loads.append(
                pltpu.make_async_copy(
                    ref.at[:, pl.ds(pl.multiple_of(row_half * columns, columns), columns),
                           pl.ds(pl.multiple_of(high * columns, columns), columns)],
                    quarters.at[gate, other],
                    local_sem.at[1 + 2 * gate + other],
                )
            )
            loads[-1].start()

    @pl.when(inner)
    def _():
        pl.semaphore_wait(barrier, 4)

    @pl.when(jnp.logical_not(inner))
    def _():
        pl.semaphore_wait(barrier, 3)


    def rows_of(j, c):
        return pl.ds(pl.multiple_of(j * block + c * tall, tall), tall)

    def rs_copy(d, j, c, src=None):
        return pltpu.make_async_remote_copy(
            src_ref=rs.at[d, j, c] if src is None else src, dst_ref=rs.at[d, j, c],
            send_sem=rs_send.at[d, j, c], recv_sem=rs_recv.at[d, j, c],
            device_id={"leaf": neighbour[d]}, device_id_type=MESH,
        )

    def core_copy(c):
        return pltpu.make_async_remote_copy(
            src_ref=ssum.at[c], dst_ref=core.at[c],
            send_sem=core_send.at[c], recv_sem=core_recv.at[c],
            device_id={"bits": partner_one}, device_id_type=MESH,
        )

    def y_copy(c):
        return pltpu.make_async_remote_copy(
            src_ref=sec.at[c], dst_ref=ybuf.at[c],
            send_sem=y_send.at[c], recv_sem=y_recv.at[c],
            device_id={"bits": partner_two}, device_id_type=MESH,
        )

    def ag_copy(d, j, c):
        piece = parts.at[:, rows_of(j, c), :]
        return pltpu.make_async_remote_copy(
            src_ref=piece, dst_ref=piece,
            send_sem=ag_send.at[d, j, c], recv_sem=ag_recv.at[d, j, c],
            device_id={"leaf": neighbour[d]}, device_id_type=MESH,
        )

    def each(count, body):
        def step(i, carry):
            body(i)
            return carry

        lax.fori_loop(0, count, step, 0)

    def product(gate, mine, theirs):
        x = jnp.concatenate([mine[0], mine[1], theirs[0], theirs[1]], axis=1)
        x_hi, x_lo = split(x)
        dot = functools.partial(jnp.dot, preferred_element_type=jnp.float32)
        return dot(x_hi, w_hi[gate]) + (dot(x_lo, w_hi[gate]) + dot(x_hi, w_lo[gate]))

    def begin(c):
        def send(k):
            @pl.when(me == 0)
            def _():
                rs_copy(0, final - k, c, state_ref.at[:, rows_of(final - k, c), :]).start()

            @pl.when(me == final)
            def _():
                rs_copy(1, k, c, state_ref.at[:, rows_of(k, c), :]).start()

        each(final, send)

    each(2, begin)

    for one in loads:
        one.wait()
    for gate in range(2):
        for other in range(2):
            re_hi, re_lo = split(quarters[gate, other, 0])
            im_hi, im_lo = split(quarters[gate, other, 1])
            top = pl.ds(2 * other * columns, columns)
            low = pl.ds((2 * other + 1) * columns, columns)
            left, right = pl.ds(0, columns), pl.ds(columns, columns)
            for w, re, im in ((w_hi, re_hi, im_hi), (w_lo, re_lo, im_lo)):
                w[gate, top, left] = re
                w[gate, top, right] = im
                w[gate, low, left] = -im
                w[gate, low, right] = re
    load.wait()

    def reduce_on(d, c):
        def toward(k):
            j, ahead = ((final - k, final - k > me), (k, k < me))[d]

            @pl.when(ahead)
            def _():
                rs_copy(d, j, c).wait_recv()
                rs[d, j, c] = rs[d, j, c] + st[:, rows_of(j, c), :]
                rs_copy(d, j, c).start()

        each(final, toward)

    def gather_near(c):
        for d, j, there in (
            (0, me - 1, (me < final) & (me > 1)), (1, me + 1, (me > 0) & (me < final - 1))
        ):

            @pl.when(there)
            def _():
                ag_copy(d, j, c).wait_recv()
                ag_copy(d, j, c).start()

    def gather_own(c):
        for d in range(2):

            @pl.when(has[d])
            def _():
                ag_copy(d, me, c).start()

    def second_step(c):
        y_copy(c).wait_recv()
        part = product(1, sec[c], ybuf[c])
        here = rows_of(me, c)
        parts[0, here, :] = part[:, :columns]
        parts[1, here, :] = part[:, columns:]

        @pl.when(inner | (c >= hold))
        def _():
            gather_own(c)

        @pl.when(jnp.logical_not(inner) & (c == hold))
        def _():
            each(hold, gather_own)

    def own_sum(c):
        @pl.when(me > 0)
        def _():
            rs_copy(0, me, c).wait_recv()

        @pl.when(me < final)
        def _():
            rs_copy(1, me, c).wait_recv()

        mine = rows_of(me, c)

        @pl.when(me == 0)
        def _():
            ssum[c] = st[:, mine, :] + rs[1, me, c]

        @pl.when(me == final)
        def _():
            ssum[c] = st[:, mine, :] + rs[0, me, c]

        @pl.when(inner)
        def _():
            ssum[c] = st[:, mine, :] + rs[0, me, c] + rs[1, me, c]

        core_copy(c).start()

    def first_step(c):
        core_copy(c).wait_recv()
        section = product(0, ssum[c], core[c])
        sec[c, 0] = section[:, :columns]
        sec[c, 1] = section[:, columns:]
        y_copy(c).start()

    def iteration(i):
        g = i - final

        @pl.when(i + 2 < CHUNKS)
        def _():
            begin(i + 2)

        @pl.when((g >= 0) & (g < CHUNKS))
        def _():
            own_sum(g)

        for d, c in ((0, g + final - me), (1, g + me)):

            @pl.when(inner & (c >= 0) & (c < CHUNKS))
            def _():
                reduce_on(d, c)

        @pl.when(g >= 4)
        def _():
            gather_near(g - 4)

        @pl.when((g >= 2) & (g < CHUNKS + 2))
        def _():
            second_step(g - 2)

        @pl.when((g >= 0) & (g < CHUNKS))
        def _():
            first_step(g)

    each(final + CHUNKS + 4, iteration)

    def gather_rest(i):
        c, k = i // n_leaf, i % n_leaf
        late = (k < me) & ((k < me - 1) | (k == 0) | (me == final))

        @pl.when(late)
        def _():
            ag_copy(0, k, c).wait_recv()

            @pl.when(me < final)
            def _():
                ag_copy(0, k, c).start()

        late_right = (k > me) & ((k > me + 1) | (k == final) | (me == 0))

        @pl.when(late_right)
        def _():
            ag_copy(1, k, c).wait_recv()

            @pl.when(me > 0)
            def _():
                ag_copy(1, k, c).start()

    each(CHUNKS * n_leaf, gather_rest)

    base = me * block
    unroll = 16

    def pick(i):
        for k in range(unroll):
            p = i * unroll + k
            row = order_ref[picks_ref[0, base + p]]
            out_ref[:, pl.ds(p, 1), :] = parts[:, pl.ds(row, 1), :]

    each(block // unroll, pick)

    def drain(i):
        c, j = i // n_leaf, i % n_leaf
        for d, sent, gathered in ((0, j > me, j <= me), (1, j < me, j >= me)):

            @pl.when(has[d] & sent)
            def _():
                rs_copy(d, j, c).wait_send()

            @pl.when(has[d] & gathered)
            def _():
                ag_copy(d, j, c).wait_send()

        @pl.when(j == 0)
        def _():
            core_copy(c).wait_send()
            y_copy(c).wait_send()

    each(CHUNKS * n_leaf, drain)


def shards(state, gate_one, gate_two, row_order, picks, counts):
    rows, columns = state.shape[-2:]
    n_leaf = lax.axis_size("leaf")
    block = rows // n_leaf
    tall = block // CHUNKS
    f32, dma = jnp.float32, pltpu.SemaphoreType.DMA
    vmem, smem, hbm = (
        pl.BlockSpec(memory_space=m) for m in (pltpu.VMEM, pltpu.SMEM, pl.ANY)
    )
    picked = pl.pallas_call(
        functools.partial(kernel, n_leaf),
        out_shape=jax.ShapeDtypeStruct((2, block, columns), f32),
        in_specs=[smem, smem, hbm, hbm, hbm],
        out_specs=vmem,
        scratch_shapes=[
            pltpu.VMEM((2, rows, columns), f32),
            pltpu.VMEM((2, n_leaf, CHUNKS, 2, tall, columns), f32),
            pltpu.VMEM((CHUNKS, 2, tall, columns), f32),
            pltpu.VMEM((CHUNKS, 2, tall, columns), f32),
            pltpu.VMEM((CHUNKS, 2, tall, columns), f32),
            pltpu.VMEM((CHUNKS, 2, tall, columns), f32),
            pltpu.VMEM((2, rows, columns), f32),
            pltpu.VMEM((2, 2, 2, columns, columns), f32),
            pltpu.VMEM((2, 4 * columns, 2 * columns), jnp.bfloat16),
            pltpu.VMEM((2, 4 * columns, 2 * columns), jnp.bfloat16),
            dma((5,)),
            dma((2, n_leaf, CHUNKS)),
            dma((2, n_leaf, CHUNKS)),
            dma((CHUNKS,)),
            dma((CHUNKS,)),
            dma((CHUNKS,)),
            dma((CHUNKS,)),
            dma((2, n_leaf, CHUNKS)),
            dma((2, n_leaf, CHUNKS)),
        ],
        compiler_params=pltpu.CompilerParams(
            collective_id=0, has_side_effects=True, vmem_limit_bytes=60 * 2**20
        ),
    )(picks, row_order, state[:, 0, 0], gate_one, gate_two)
    live_counts = lax.dynamic_slice_in_dim(counts[0], lax.axis_index("leaf") * block, block)
    keep_mask = jnp.arange(columns, dtype=jnp.int32)[None, :] < live_counts[:, None]
    return jnp.where(keep_mask[None], picked, jnp.zeros_like(picked))[:, None]


def solution(mesh):
    return jax.shard_map(
        shards,
        mesh=mesh,
        in_specs=(
            P(None, "leaf", "bits", None, None),
            P(),
            P(),
            P(),
            P("bits", None),
            P("bits", None),
        ),
        out_specs=P(None, "bits", "leaf", None),
        check_vma=False,
    )
```
